256 devices in a mesh: mem: 16 (over z, core), reg: 16 (over x, y).
Axes of the slice: x: 4, y: 4, z: 8, core: 2. Of those that a mesh axis runs over, the one named last changes fastest.
Arguments:
- anomalies: bfloat16 [1024, 262144], P('mem', 'reg'), may hold values from -6 to 6
- obs_anomalies: bfloat16 [1024, 8192], P('mem', 'reg'), may hold values from -6 to 6
- innovations: bfloat16 [1024, 8192], P('mem', 'reg'), may hold values from -6 to 6
- obs_links: int32 [2048, 12], P('reg'), may hold values from 0 to 19, as said below
- taper_choice: int32 [2048, 12], P('reg'), may hold values from 0 to 7
- tapers: float32 [8, 128, 128], replicated, may hold values from 0.1 to 1
Outputs:
- increments: bfloat16 [1024, 262144], P('mem', 'reg')
The draws below stay inside these ranges and needn't reach their ends.
Inputs may be any that keep to these rules, and one draw needn't show every extreme that they name: `obs_links`: each row names 12 different positions of a window of 20 observation blocks: position w is block w mod 4 of region r + w // 4 - 2 (regions counted cyclically), r being the state block's region.
All inputs are finite; a program needn't handle non-finite values.
Results may differ from the reference program's by a relative error of at most 0.005.
Values may be sent and summed in bfloat16 or wider, within the bound.
No kernel may reach another device: no remote copies, remote signals or barrier semaphores. Data moves between devices by JAX's collectives and lax.ppermute only.
A program may use at most 128 MiB of HBM per device.

```python
import jax
import jax.numpy as jnp
from jax import lax

MEMBERS = 1024
BLK = 128
LINKS = 12
NTAPER = 8
SBLK_REG = 128
OBLK_REG = 4
NSB = 2048
NOB = 64
NSTATE = 262144
NOBS = 8192


def draw_obs_links(key, part):
    window_len = 5 * OBLK_REG
    row_keys = jax.random.split(key, NSB)
    scores = jax.vmap(lambda row_key: jax.random.permutation(row_key, window_len))(row_keys).astype(jnp.int32)
    scores = scores.at[0, 0].set(-2).at[0, window_len - 1].set(-1)
    ranking = jnp.argsort(scores, axis=1, stable=True)
    return ranking[:, :LINKS].astype(jnp.int32)


def plant(drawn, stream_key, least, high):
    dims = drawn.shape
    place = [jax.random.randint(jax.random.fold_in(stream_key, axis), (), 0, dims[axis]) for axis in range(len(dims))]
    drawn = drawn.at[tuple(place)].set(least)
    longest = dims.index(max(dims))
    place[longest] = (place[longest] + 1) % dims[longest]
    return drawn.at[tuple(place)].set(high)


def shard_levels(key, dims, pieces, low, largest):
    level, own = 1.0, jax.random.fold_in(key, 6)
    for dim, blocks in pieces:
        heights = jnp.exp(jax.random.uniform(jax.random.fold_in(own, dim), (blocks,), jnp.float32, low / len(pieces), largest / len(pieces)))
        level = level * jnp.repeat(heights, dims[dim] // blocks).reshape([-1 if axis == dim else 1 for axis in range(len(dims))])
    return level


def bell_draw(rng, extent, width, limit, pieces=(), held_as=jnp.bfloat16):
    entries = jax.random.normal(rng, extent, jnp.float32) * width
    if len(pieces) > 0:
        entries = shard_levels(rng, extent, pieces, -0.22, 0.18) * entries
    return jnp.clip(entries, min=-limit, max=limit).astype(held_as)


def setup_inputs(seed: int = 0) -> dict:
    arg_keys = jax.random.split(jax.random.key(seed), 7)
    return {
        "anomalies": bell_draw(arg_keys[0], (MEMBERS, NSTATE), 1.0, 6.0, ((0, 16), (1, 16))),
        "obs_anomalies": bell_draw(arg_keys[1], (MEMBERS, NOBS), 1.0, 6.0, ((0, 16), (1, 16))),
        "innovations": bell_draw(arg_keys[2], (MEMBERS, NOBS), 1.0, 6.0, ((0, 16), (1, 16))),
        "obs_links": draw_obs_links(jax.random.fold_in(arg_keys[6], 71), 0),
        "taper_choice": plant(jax.random.randint(arg_keys[4], (NSB, LINKS), 0, NTAPER), jax.random.fold_in(arg_keys[4], 1), 0, NTAPER - 1).astype(jnp.int32),
        "tapers": jnp.clip(jax.random.uniform(arg_keys[5], (NTAPER, BLK, BLK), jnp.float32, 0.1, 1.0), 0.1, 1.0),
    }


def reference(anomalies, obs_anomalies, innovations, obs_links, taper_choice, tapers):
    region = jnp.arange(NSB, dtype=jnp.int32) // SBLK_REG
    global_ids = ((region[:, None] * OBLK_REG - 2 * OBLK_REG + obs_links) % NOB).astype(jnp.int32)
    state_blocks = anomalies.reshape(MEMBERS, NSB, BLK)
    obs_blocks = obs_anomalies.reshape(MEMBERS, NOB, BLK)
    innov_blocks = innovations.reshape(MEMBERS, NOB, BLK)

    def single_block(block_index):
        state_block = lax.dynamic_index_in_dim(state_blocks, block_index, 1, keepdims=False).astype(jnp.float32)
        chosen_ids = global_ids[block_index]
        chosen_obs = jnp.take(obs_blocks, chosen_ids, axis=1).reshape(MEMBERS, LINKS * BLK).astype(jnp.float32)
        chosen_innov = jnp.take(innov_blocks, chosen_ids, axis=1).reshape(MEMBERS, LINKS * BLK).astype(jnp.float32)
        covariance = jnp.dot(state_block.T, chosen_obs, preferred_element_type=jnp.float32) / (MEMBERS - 1)
        taper_tiles = jnp.take(tapers, taper_choice[block_index], axis=0).transpose(1, 0, 2).reshape(BLK, LINKS * BLK)
        tapered = lax.optimization_barrier((covariance * taper_tiles).astype(jnp.bfloat16))
        return jnp.dot(chosen_innov, tapered.astype(jnp.float32).T, preferred_element_type=jnp.float32).astype(jnp.bfloat16)

    result = lax.map(single_block, jnp.arange(NSB, dtype=jnp.int32))
    return result.transpose(1, 0, 2).reshape(MEMBERS, NSB * BLK)
```

```python
import functools

import jax
import jax.numpy as jnp
from jax import lax
from jax.experimental import pallas as pl
from jax.experimental.pallas import tpu as pltpu
from jax.sharding import PartitionSpec as P

BLK = 128

RING = (0, 1, 2, 3, 4, -1, -2, -3)


def along_z(x, by):
    size = lax.axis_size("mem")
    return lax.ppermute(x, "mem", [(i, (i + 2 * by) % size) for i in range(size)])


def other_core(x):
    size = lax.axis_size("mem")
    return lax.ppermute(x, "mem", [(i, i ^ 1) for i in range(size)])


def along_reg(x, by):
    size = lax.axis_size("reg")
    return lax.ppermute(x, "reg", [(i, (i + by) % size) for i in range(size)])


def ring_slices(x):
    up, down = [x], [x]
    for step in range(4):
        above = along_z(up[-1], 1)
        if step < 3:
            below = along_z(down[-1], -1)
            above, below = lax.optimization_barrier((above, below))
            down.append(below)
        up.append(above)
    return up + down[1:]


def body(scal, tapers, patches, *refs):
    n = (len(refs) - 8) // 4
    obs_hbm = refs[: 2 * n]
    innov_hbm = refs[2 * n : 4 * n]
    out, obs, innov, rows, cols, tapered, scaled, sems = refs[4 * n :]
    copies = []
    for k in range(2 * n):
        copies.append(pltpu.make_async_copy(obs_hbm[k], obs.at[k], sems.at[k]))
    for k in range(2 * n):
        copies.append(pltpu.make_async_copy(innov_hbm[k], innov.at[k], sems.at[2 * n + k]))
    for copy in copies:
        copy.start()
    z = scal[0]
    core = scal[1]
    width = patches.shape[-1]
    half = 8 * 64
    scaled[...] = tapers[...] * (1.0 / 1023.0)
    for h in range(2):
        for j in range(8):
            rows[pl.ds(h * half + j * 64, 64), :] = patches[(z - RING[j]) & 7, core ^ h]

    def turn(k, carry):
        at = pl.multiple_of(k * BLK, BLK)
        cols[:, pl.ds(at, BLK)] = rows[pl.ds(at, BLK), :].T
        return carry

    lax.fori_loop(0, 2 * half // BLK, turn, 0)
    for copy in copies[: 2 * n]:
        copy.wait()

    def cover(step, carry):
        piece = step // 2
        at = pl.multiple_of((step % 2) * 256, 256)
        to = pl.multiple_of(step * 256, 256)
        y0 = obs[2 * piece, :, :, pl.ds(at, 256)].reshape(half, 256)
        y1 = obs[2 * piece + 1, :, :, pl.ds(at, 256)].reshape(half, 256)
        cov = jnp.dot(cols[:, :half], y0, preferred_element_type=jnp.float32)
        cov += jnp.dot(cols[:, half:], y1, preferred_element_type=jnp.float32)
        for b in range(width // BLK):
            for w in range(2):
                t = scal[2 + b * 20 + step * 2 + w]
                tile = cov[b * BLK : (b + 1) * BLK, w * BLK : (w + 1) * BLK]
                tile = tile * scaled[jnp.maximum(t, 0)]
                tile = jnp.where(t >= 0, tile, 0.0)
                tapered[pl.ds(b * BLK, BLK), pl.ds(to + w * BLK, BLK)] = tile.astype(jnp.bfloat16)
        return carry

    lax.fori_loop(0, 2 * n, cover, 0)
    for copy in copies[2 * n :]:
        copy.wait()

    def spread(step, carry):
        h = step // (width // 256)
        at = pl.multiple_of((step % (width // 256)) * 256, 256)
        total = jnp.zeros((half, 256), jnp.float32)
        for piece in range(n):
            total += lax.dot_general(
                innov[2 * piece + h].reshape(half, 512),
                tapered[pl.ds(at, 256), pl.ds(piece * 512, 512)],
                (((1,), (1,)), ((), ())),
                preferred_element_type=jnp.float32,
            )
        rounded = total.astype(jnp.bfloat16)
        for j in range(8):
            out[(z - RING[j]) & 7, core ^ h, :, pl.ds(at, 256)] = rounded[j * 64 : (j + 1) * 64]
        return carry

    lax.fori_loop(0, 2 * (width // 256), spread, 0)


def analyse(scal, tapers, patches, obs_pieces, innov_pieces):
    n = len(obs_pieces)
    vmem = pl.BlockSpec(memory_space=pltpu.VMEM)
    hbm = pl.BlockSpec(memory_space=pl.ANY)
    width = patches.shape[-1]
    return pl.pallas_call(
        body,
        out_shape=jax.ShapeDtypeStruct(patches.shape, jnp.bfloat16),
        in_specs=[pl.BlockSpec(memory_space=pltpu.SMEM), vmem, vmem] + [hbm] * (2 * n),
        out_specs=vmem,
        scratch_shapes=[
            pltpu.VMEM((n, 8, 64, 512), jnp.bfloat16),
            pltpu.VMEM((n, 8, 64, 512), jnp.bfloat16),
            pltpu.VMEM((1024, width), jnp.bfloat16),
            pltpu.VMEM((width, 1024), jnp.bfloat16),
            pltpu.VMEM((width, 2560), jnp.bfloat16),
            pltpu.VMEM(tapers.shape, jnp.float32),
            pltpu.SemaphoreType.DMA((2 * n,)),
        ],
        compiler_params=pltpu.CompilerParams(vmem_limit_bytes=40 << 20),
        cost_estimate=pl.CostEstimate(flops=11 * 10**9, bytes_accessed=15 << 20, transcendentals=0),
        name="analyse",
    )(scal, tapers, patches, *obs_pieces, *innov_pieces)


def window(own):
    first = [along_reg(own, 1), along_reg(own, -1)]
    second = [along_reg(first[0], 1), along_reg(first[1], -1)]
    pieces = []
    for piece in (second[0], first[0], own, first[1], second[1]):
        pieces += [piece, other_core(piece)]
    return pieces


def local(anomalies, obs_anomalies, innovations, obs_links, taper_choice, tapers):
    mem_dev, state_cols = anomalies.shape
    mem_count = lax.axis_size("mem")
    per_dev = state_cols // BLK // mem_count
    me = lax.axis_index("mem")

    slices = ring_slices(jnp.concatenate([obs_anomalies, innovations], axis=1))
    obs_own = jnp.stack([s[:, :512] for s in slices])
    innov_own = jnp.stack([s[:, 512:] for s in slices])

    sent = anomalies.reshape(mem_dev, mem_count, per_dev * BLK).transpose(1, 0, 2)
    sent, _ = lax.optimization_barrier((sent, slices[4]))
    patches = lax.all_to_all(sent, "mem", split_axis=0, concat_axis=0, tiled=True)
    patches = patches.reshape(mem_count // 2, 2, mem_dev, per_dev * BLK)

    obs_pieces = window(obs_own)
    innov_pieces = window(innov_own)

    my_links = lax.dynamic_slice_in_dim(obs_links, me * per_dev, per_dev, 0)
    my_choice = lax.dynamic_slice_in_dim(taper_choice, me * per_dev, per_dev, 0)
    places = jnp.arange(20, dtype=jnp.int32)
    hit = my_links[:, :, None] == places[None, None, :]
    table = jnp.max(jnp.where(hit, my_choice[:, :, None], -1), axis=1)
    scal = jnp.concatenate([jnp.stack([me // 2, me % 2]).astype(jnp.int32), table.reshape(-1)])

    result = analyse(scal, tapers, patches, obs_pieces, innov_pieces)
    result = result.reshape(mem_count, mem_dev, per_dev * BLK)
    returned = lax.all_to_all(result, "mem", split_axis=0, concat_axis=0, tiled=True)
    return returned.transpose(1, 0, 2).reshape(mem_dev, state_cols)


def solution(mesh):
    return jax.shard_map(
        local,
        mesh=mesh,
        in_specs=(
            P("mem", "reg"),
            P("mem", "reg"),
            P("mem", "reg"),
            P("reg", None),
            P("reg", None),
            P(),
        ),
        out_specs=P("mem", "reg"),
        check_vma=False,
    )
```

```python
import jax
import jax.numpy as jnp
from jax import lax
from jax.experimental import pallas as pl
from jax.experimental.pallas import tpu as pltpu
from jax.sharding import PartitionSpec as P

BLK = 128

RING = (0, 1, -1, 2, -2, 3, -3, 4)


def along_z(x, by):
    size = lax.axis_size("mem")
    return lax.ppermute(x, "mem", [(i, (i + 2 * by) % size) for i in range(size)])


def other_core(x):
    size = lax.axis_size("mem")
    return lax.ppermute(x, "mem", [(i, i ^ 1) for i in range(size)])


def along_reg(x, by):
    size = lax.axis_size("reg")
    return lax.ppermute(x, "reg", [(i, (i + by) % size) for i in range(size)])


def gather_other(core_ref, anomalies, out, sems):
    z = core_ref[0]
    core = core_ref[1]
    width = out.shape[-1]
    copies = []
    for j, d in enumerate(RING):
        at = pl.multiple_of((((z + d) & 7) * 2 + (1 - core)) * width, width)
        copies.append(pltpu.make_async_copy(anomalies.at[:, pl.ds(at, width)], out.at[j], sems.at[j]))
    for copy in copies:
        copy.start()
    for copy in copies:
        copy.wait()


def gather_both(core_ref, anomalies, other, *refs):
    outs, sems = refs[:8], refs[8]
    z = core_ref[0]
    core = core_ref[1]
    width = other.shape[-1]
    copies = []
    for j, d in enumerate(RING):
        at = pl.multiple_of((((z + d) & 7) * 2 + core) * width, width)
        copies.append(pltpu.make_async_copy(anomalies.at[:, pl.ds(at, width)], outs[j].at[0], sems.at[j]))
    for copy in copies:
        copy.start()
    for j in range(8):
        outs[j][1] = other[j]
    for copy in copies:
        copy.wait()


def messages(place, anomalies, width):
    rows = anomalies.shape[0]
    smem = pl.BlockSpec(memory_space=pltpu.SMEM)
    vmem = pl.BlockSpec(memory_space=pltpu.VMEM)
    hbm = pl.BlockSpec(memory_space=pltpu.HBM)
    other = pl.pallas_call(
        gather_other,
        out_shape=jax.ShapeDtypeStruct((8, rows, width), jnp.bfloat16),
        in_specs=[smem, hbm],
        out_specs=vmem,
        scratch_shapes=[pltpu.SemaphoreType.DMA((8,))],
        compiler_params=pltpu.CompilerParams(vmem_limit_bytes=4 << 20),
        cost_estimate=pl.CostEstimate(flops=0, bytes_accessed=2 << 20, transcendentals=0),
        name="gather_other",
    )(place, anomalies)
    other = other_core(other)
    return pl.pallas_call(
        gather_both,
        out_shape=[jax.ShapeDtypeStruct((2, rows, width), jnp.bfloat16)] * 8,
        in_specs=[smem, hbm, vmem],
        out_specs=[vmem] * 8,
        scratch_shapes=[pltpu.SemaphoreType.DMA((8,))],
        compiler_params=pltpu.CompilerParams(vmem_limit_bytes=6 << 20),
        cost_estimate=pl.CostEstimate(flops=0, bytes_accessed=4 << 20, transcendentals=0),
        name="gather_both",
    )(place, anomalies, other)


def body(scal, tapers, *refs):
    patches = refs[:8]
    windows = refs[8:28]
    out, held, obs, innov, cols, tapered, scaled, done, in_sems, out_sems = refs[28:]
    z = scal[0]
    core = scal[1]
    width = cols.shape[0]
    slices = obs.shape[1]
    count = obs.shape[-1]
    depth = slices * 64
    copies = [pltpu.make_async_copy(patches[j], held.at[j], in_sems.at[j]) for j in range(8)]
    obs_copies = [
        pltpu.make_async_copy(windows[k].at[:, :, pl.ds(0, count)], obs.at[k], in_sems.at[8 + k]) for k in range(20)
    ]
    innov_copies = [
        pltpu.make_async_copy(windows[k].at[:, :, pl.ds(count, count)], innov.at[k], in_sems.at[28 + k])
        for k in range(20)
    ]
    for copy in copies + obs_copies[:4]:
        copy.start()
    scaled[pl.ds(0, 8)] = tapers[...] * (1.0 / 1023.0)
    scaled[8] = jnp.zeros((BLK, BLK), jnp.float32)
    for k in range(4):
        copies[2 * k].wait()
        copies[2 * k + 1].wait()
        for copy in obs_copies[4 * k + 4 : 4 * k + 8]:
            copy.start()
        for h in range(2):
            pair = jnp.concatenate([held[2 * k, h], held[2 * k + 1, h]], axis=0)
            cols[:, pl.ds((4 * h + k) * BLK, BLK)] = pair.T
    for k in range(4):
        for region in range(5):
            innov_copies[4 * region + k].start()

    for region in range(5):
        for copy in obs_copies[4 * region : 4 * region + 4]:
            copy.wait()
        for half in range(2):
            cov = jnp.zeros((width, 256), jnp.float32)
            for k in range(4):
                y = obs[4 * region + k, :, :, pl.ds(half * 256, 256)].reshape(depth, 256)
                cov += jnp.dot(cols[:, pl.ds(k * depth, depth)], y, preferred_element_type=jnp.float32)
            for b in range(width // BLK):
                for w in range(2):
                    at = region * 512 + half * 256 + w * BLK
                    t = scal[8 + b * 20 + at // BLK]
                    tile = cov[b * BLK : (b + 1) * BLK, w * BLK : (w + 1) * BLK] * scaled[t]
                    tapered[pl.ds(b * BLK, BLK), pl.ds(at, BLK)] = tile.astype(jnp.bfloat16)

    out_copies = []
    for k in range(4):
        for region in range(5):
            innov_copies[4 * region + k].wait()
        for at in range(0, width, 256):
            total = jnp.zeros((depth, 256), jnp.float32)
            for region in range(5):
                total += lax.dot_general(
                    innov[4 * region + k].reshape(depth, count),
                    tapered[pl.ds(at, 256), pl.ds(region * count, count)],
                    (((1,), (1,)), ((), ())),
                    preferred_element_type=jnp.float32,
                )
            done[pl.ds(k * slices, slices), :, pl.ds(at, 256)] = total.astype(jnp.bfloat16).reshape(slices, 64, 256)
        for i in range(slices):
            j, h = (k % 2) * slices + i, k // 2
            copy = pltpu.make_async_copy(
                done.at[k * slices + i], out.at[(z - RING[j]) & 7, core ^ h], out_sems.at[k * slices + i]
            )
            copy.start()
            out_copies.append(copy)
    for copy in out_copies:
        copy.wait()


def analyse(scal, tapers, patches, windows):
    smem = pl.BlockSpec(memory_space=pltpu.SMEM)
    vmem = pl.BlockSpec(memory_space=pltpu.VMEM)
    hbm = pl.BlockSpec(memory_space=pltpu.HBM)
    members, width = patches[0].shape[1:]
    slices = windows[0].shape[0]
    return pl.pallas_call(
        body,
        out_shape=jax.ShapeDtypeStruct((8, 2, members, width), jnp.bfloat16),
        in_specs=[smem, vmem] + [hbm] * 28,
        out_specs=hbm,
        scratch_shapes=[
            pltpu.VMEM((8, 2, members, width), jnp.bfloat16),
            pltpu.VMEM((20, slices, members, 512), jnp.bfloat16),
            pltpu.VMEM((20, slices, members, 512), jnp.bfloat16),
            pltpu.VMEM((width, 1024), jnp.bfloat16),
            pltpu.VMEM((width, 2560), jnp.bfloat16),
            pltpu.VMEM((9, BLK, BLK), jnp.float32),
            pltpu.VMEM((16, members, width), jnp.bfloat16),
            pltpu.SemaphoreType.DMA((48,)),
            pltpu.SemaphoreType.DMA((16,)),
        ],
        compiler_params=pltpu.CompilerParams(vmem_limit_bytes=24 << 20),
        cost_estimate=pl.CostEstimate(flops=11 * 10**9, bytes_accessed=15 << 20, transcendentals=0),
        name="analyse",
    )(scal, tapers, *patches, *windows)


def step(anomalies, obs_anomalies, innovations, obs_links, taper_choice, tapers):
    mem_dev, state_cols = anomalies.shape
    mem_count = lax.axis_size("mem")
    per_dev = state_cols // BLK // mem_count
    width = per_dev * BLK
    me = lax.axis_index("mem")
    place = jnp.stack([me // 2, me % 2]).astype(jnp.int32)

    own = jnp.concatenate([obs_anomalies, innovations], axis=1)
    sent = messages(place, anomalies, width)
    up1, down1 = along_z(own, 1), along_z(own, -1)
    up2, down2 = along_z(up1, 1), along_z(down1, -1)
    up3, down3 = along_z(up2, 1), along_z(down2, -1)
    down4 = along_z(down3, -1)
    patches = [sent[0]] + [along_z(sent[j], RING[j]) for j in range(1, 8)]

    a0 = jnp.stack([own, up1, down1, up2])
    b0 = jnp.stack([down2, up3, down3, down4])
    a_up, a_down = along_reg(a0, 1), along_reg(a0, -1)
    b_up, b_down = along_reg(b0, 1), along_reg(b0, -1)
    a_up2, a_down2 = along_reg(a_up, 1), along_reg(a_down, -1)
    b_up2, b_down2 = along_reg(b_up, 1), along_reg(b_down, -1)
    windows = []
    for a, b in ((a_up2, b_up2), (a_up, b_up), (a0, b0), (a_down, b_down), (a_down2, b_down2)):
        windows += [a, b, other_core(a), other_core(b)]

    my_links = lax.dynamic_slice_in_dim(obs_links, me * per_dev, per_dev, 0)
    my_choice = lax.dynamic_slice_in_dim(taper_choice, me * per_dev, per_dev, 0)
    places = jnp.arange(20, dtype=jnp.int32)
    missed = my_links[:, :, None] != places[None, None, :]
    table = jnp.min(jnp.where(missed, 8, my_choice[:, :, None]), axis=1).reshape(-1)

    scal = jnp.concatenate([place, jnp.zeros((6,), jnp.int32), table])
    result = analyse(scal, tapers, patches, windows).reshape(mem_count, mem_dev, width)
    returned = lax.all_to_all(result, "mem", split_axis=0, concat_axis=0, tiled=True)
    return returned.transpose(1, 0, 2).reshape(mem_dev, state_cols)


def solution(mesh):
    return jax.shard_map(
        step,
        mesh=mesh,
        in_specs=(
            P("mem", "reg"),
            P("mem", "reg"),
            P("mem", "reg"),
            P("reg", None),
            P("reg", None),
            P(),
        ),
        out_specs=P("mem", "reg"),
        check_vma=False,
    )
```

```python
import functools

import jax
import jax.numpy as jnp
from jax import lax
from jax.experimental import pallas as pl
from jax.experimental.pallas import tpu as pltpu
from jax.sharding import PartitionSpec as P

BLK = 128
PARTS = 2

RING = (0, 1, -1, 2, -2, 3, -3, 4)


def along_z(x, by):
    size = lax.axis_size("mem")
    return lax.ppermute(x, "mem", [(i, (i + 2 * by) % size) for i in range(size)])


def other_core(x):
    size = lax.axis_size("mem")
    return lax.ppermute(x, "mem", [(i, i ^ 1) for i in range(size)])


def along_reg(x, by):
    size = lax.axis_size("reg")
    return lax.ppermute(x, "reg", [(i, (i + by) % size) for i in range(size)])


def gather_other(core_ref, anomalies, out, sems):
    z = core_ref[0]
    core = core_ref[1]
    width = out.shape[-1]
    copies = []
    for j, d in enumerate(RING):
        at = pl.multiple_of((((z + d) & 7) * 2 + (1 - core)) * width, width)
        copies.append(pltpu.make_async_copy(anomalies.at[:, pl.ds(at, width)], out.at[j], sems.at[j]))
    for copy in copies:
        copy.start()
    for copy in copies:
        copy.wait()


def gather_both(core_ref, anomalies, other, *refs):
    outs, sems = refs[:8], refs[8]
    z = core_ref[0]
    core = core_ref[1]
    width = other.shape[-1]
    copies = []
    for j, d in enumerate(RING):
        at = pl.multiple_of((((z + d) & 7) * 2 + core) * width, width)
        copies.append(pltpu.make_async_copy(anomalies.at[:, pl.ds(at, width)], outs[j].at[0], sems.at[j]))
    for copy in copies:
        copy.start()
    for j in range(8):
        outs[j][1] = other[j]
    for copy in copies:
        copy.wait()


def messages(place, anomalies, width):
    rows = anomalies.shape[0]
    smem = pl.BlockSpec(memory_space=pltpu.SMEM)
    vmem = pl.BlockSpec(memory_space=pltpu.VMEM)
    hbm = pl.BlockSpec(memory_space=pltpu.HBM)
    other = pl.pallas_call(
        gather_other,
        out_shape=jax.ShapeDtypeStruct((8, rows, width), jnp.bfloat16),
        in_specs=[smem, hbm],
        out_specs=vmem,
        scratch_shapes=[pltpu.SemaphoreType.DMA((8,))],
        compiler_params=pltpu.CompilerParams(vmem_limit_bytes=4 << 20),
        cost_estimate=pl.CostEstimate(flops=0, bytes_accessed=2 << 20, transcendentals=0),
        name="gather_other",
    )(place, anomalies)
    other = other_core(other)
    return pl.pallas_call(
        gather_both,
        out_shape=[jax.ShapeDtypeStruct((2, rows, width), jnp.bfloat16)] * 8,
        in_specs=[smem, hbm, vmem],
        out_specs=[vmem] * 8,
        scratch_shapes=[pltpu.SemaphoreType.DMA((8,))],
        compiler_params=pltpu.CompilerParams(vmem_limit_bytes=6 << 20),
        cost_estimate=pl.CostEstimate(flops=0, bytes_accessed=4 << 20, transcendentals=0),
        name="gather_both",
    )(place, anomalies, other)


def body(part, scal, tapers, *refs):
    patches = refs[:8]
    windows = refs[8:28]
    out, held, obs, innov, cols, tapered, scaled, done, in_sems, out_sems = refs[28:]
    z = scal[0]
    core = scal[1]
    width = cols.shape[0]
    slices = obs.shape[1]
    count = obs.shape[-1]
    depth = slices * 64
    mine = pl.ds(part * width, width)
    copies = [pltpu.make_async_copy(patches[j].at[:, :, mine], held.at[j], in_sems.at[j]) for j in range(8)]
    obs_copies = [
        pltpu.make_async_copy(windows[k].at[:, :, pl.ds(0, count)], obs.at[k], in_sems.at[8 + k]) for k in range(20)
    ]
    innov_copies = [
        pltpu.make_async_copy(windows[k].at[:, :, pl.ds(count, count)], innov.at[k], in_sems.at[28 + k])
        for k in range(20)
    ]
    for copy in copies + obs_copies[:4]:
        copy.start()
    scaled[pl.ds(0, 8)] = tapers[...] * (1.0 / 1023.0)
    scaled[8] = jnp.zeros((BLK, BLK), jnp.float32)
    for k in range(4):
        copies[2 * k].wait()
        copies[2 * k + 1].wait()
        for copy in obs_copies[4 * k + 4 : 4 * k + 8]:
            copy.start()
        for h in range(2):
            pair = jnp.concatenate([held[2 * k, h], held[2 * k + 1, h]], axis=0)
            cols[:, pl.ds((4 * h + k) * BLK, BLK)] = pair.T
    for k in range(4):
        for region in range(5):
            innov_copies[4 * region + k].start()

    for region in range(5):
        for copy in obs_copies[4 * region : 4 * region + 4]:
            copy.wait()
        for half in range(2):
            cov = jnp.zeros((width, 256), jnp.float32)
            for k in range(4):
                y = obs[4 * region + k, :, :, pl.ds(half * 256, 256)].reshape(depth, 256)
                cov += jnp.dot(cols[:, pl.ds(k * depth, depth)], y, preferred_element_type=jnp.float32)
            for b in range(width // BLK):
                for w in range(2):
                    at = region * 512 + half * 256 + w * BLK
                    t = scal[8 + (part * (width // BLK) + b) * 20 + at // BLK]
                    tile = cov[b * BLK : (b + 1) * BLK, w * BLK : (w + 1) * BLK] * scaled[t]
                    tapered[pl.ds(b * BLK, BLK), pl.ds(at, BLK)] = tile.astype(jnp.bfloat16)

    out_copies = []
    for k in range(4):
        for region in range(5):
            innov_copies[4 * region + k].wait()
        for at in range(0, width, 256):
            total = jnp.zeros((depth, 256), jnp.float32)
            for region in range(5):
                total += lax.dot_general(
                    innov[4 * region + k].reshape(depth, count),
                    tapered[pl.ds(at, 256), pl.ds(region * count, count)],
                    (((1,), (1,)), ((), ())),
                    preferred_element_type=jnp.float32,
                )
            done[pl.ds(k * slices, slices), :, pl.ds(at, 256)] = total.astype(jnp.bfloat16).reshape(slices, 64, 256)
        for i in range(slices):
            j, h = (k % 2) * slices + i, k // 2
            copy = pltpu.make_async_copy(
                done.at[k * slices + i], out.at[(z - RING[j]) & 7, core ^ h], out_sems.at[k * slices + i]
            )
            copy.start()
            out_copies.append(copy)
    for copy in out_copies:
        copy.wait()


def analyse(part, scal, tapers, patches, windows):
    smem = pl.BlockSpec(memory_space=pltpu.SMEM)
    vmem = pl.BlockSpec(memory_space=pltpu.VMEM)
    hbm = pl.BlockSpec(memory_space=pltpu.HBM)
    members, width = patches[0].shape[1], patches[0].shape[2] // PARTS
    slices = windows[0].shape[0]
    return pl.pallas_call(
        functools.partial(body, part),
        out_shape=jax.ShapeDtypeStruct((8, 2, members, width), jnp.bfloat16),
        in_specs=[smem, vmem] + [hbm] * 28,
        out_specs=hbm,
        scratch_shapes=[
            pltpu.VMEM((8, 2, members, width), jnp.bfloat16),
            pltpu.VMEM((20, slices, members, 512), jnp.bfloat16),
            pltpu.VMEM((20, slices, members, 512), jnp.bfloat16),
            pltpu.VMEM((width, 1024), jnp.bfloat16),
            pltpu.VMEM((width, 2560), jnp.bfloat16),
            pltpu.VMEM((9, BLK, BLK), jnp.float32),
            pltpu.VMEM((16, members, width), jnp.bfloat16),
            pltpu.SemaphoreType.DMA((48,)),
            pltpu.SemaphoreType.DMA((16,)),
        ],
        compiler_params=pltpu.CompilerParams(vmem_limit_bytes=56 << 20),
        cost_estimate=pl.CostEstimate(flops=11 * 10**9 // PARTS, bytes_accessed=15 << 20, transcendentals=0),
        name="analyse",
    )(scal, tapers, *patches, *windows)


def step(anomalies, obs_anomalies, innovations, obs_links, taper_choice, tapers):
    mem_dev, state_cols = anomalies.shape
    mem_count = lax.axis_size("mem")
    per_dev = state_cols // BLK // mem_count
    width = per_dev * BLK
    me = lax.axis_index("mem")
    place = jnp.stack([me // 2, me % 2]).astype(jnp.int32)

    own = jnp.concatenate([obs_anomalies, innovations], axis=1)
    sent = messages(place, anomalies, width)
    up1, down1 = along_z(own, 1), along_z(own, -1)
    up2, down2 = along_z(up1, 1), along_z(down1, -1)
    up3, down3 = along_z(up2, 1), along_z(down2, -1)
    down4 = along_z(down3, -1)
    patches = [sent[0]] + [along_z(sent[j], RING[j]) for j in range(1, 8)]

    a0 = jnp.stack([own, up1, down1, up2])
    b0 = jnp.stack([down2, up3, down3, down4])
    a_up, a_down = along_reg(a0, 1), along_reg(a0, -1)
    b_up, b_down = along_reg(b0, 1), along_reg(b0, -1)
    a_up2, a_down2 = along_reg(a_up, 1), along_reg(a_down, -1)
    b_up2, b_down2 = along_reg(b_up, 1), along_reg(b_down, -1)
    windows = []
    for a, b in ((a_up2, b_up2), (a_up, b_up), (a0, b0), (a_down, b_down), (a_down2, b_down2)):
        windows += [a, b, other_core(a), other_core(b)]

    my_links = lax.dynamic_slice_in_dim(obs_links, me * per_dev, per_dev, 0)
    my_choice = lax.dynamic_slice_in_dim(taper_choice, me * per_dev, per_dev, 0)
    places = jnp.arange(20, dtype=jnp.int32)
    missed = my_links[:, :, None] != places[None, None, :]
    table = jnp.min(jnp.where(missed, 8, my_choice[:, :, None]), axis=1).reshape(-1)

    scal = jnp.concatenate([place, jnp.zeros((6,), jnp.int32), table])
    returned = []
    for part in range(PARTS):
        result = analyse(part, scal, tapers, patches, windows).reshape(mem_count, mem_dev, width // PARTS)
        returned.append(lax.all_to_all(result, "mem", split_axis=0, concat_axis=0, tiled=True))
    whole = jnp.concatenate(returned, axis=2)
    return whole.transpose(1, 0, 2).reshape(mem_dev, state_cols)


def solution(mesh):
    return jax.shard_map(
        step,
        mesh=mesh,
        in_specs=(
            P("mem", "reg"),
            P("mem", "reg"),
            P("mem", "reg"),
            P("reg", None),
            P("reg", None),
            P(),
        ),
        out_specs=P("mem", "reg"),
        check_vma=False,
    )
```
